32 devices in a mesh: dp: 8 (over z, x), tensor: 4 (over y, core).
Axes of the slice: x: 2, y: 2, z: 4, core: 2. Of those that a mesh axis runs over, the one named last changes fastest.
Arguments:
- layer_entry_rows: bfloat16 [64, 64, 768], P('dp'), may hold values from -6 to 6
- frozen_picture_features: bfloat16 [64, 257, 1408], P('dp'), may hold values from -6 to 6
- caption_sizes: int32 [64], P('dp'), may hold values from 5 to 32, as said below
- inner_attend_projectors: bfloat16 [768, 3, 768], P(None, None, 'tensor'), may hold values from -0.21875 to 0.21875
- inner_attend_offsets: bfloat16 [2, 768], P(None, 'tensor'), may hold values from -3 to 3
- inner_attend_exit_matrix: bfloat16 [768, 768], P('tensor'), may hold values from -0.875 to 0.875
- inner_attend_exit_offset: bfloat16 [768], replicated, may hold values from -3 to 3
- mutual_attend_probe_matrix: bfloat16 [768, 768], P(None, 'tensor'), may hold values from -0.21875 to 0.21875
- picture_keyvalue_matrix: bfloat16 [1408, 2, 768], P(None, None, 'tensor'), may hold values from -0.15625 to 0.15625
- mutual_attend_offsets: bfloat16 [2, 768], P(None, 'tensor'), may hold values from -3 to 3
- mutual_attend_exit_matrix: bfloat16 [768, 768], P('tensor'), may hold values from -1.75 to 1.75
- mutual_attend_exit_offset: bfloat16 [768], replicated, may hold values from -3 to 3
- expansion_matrices: bfloat16 [2, 768, 3072], P(None, None, 'tensor'), may hold values from -0.21875 to 0.21875
- expansion_offsets: bfloat16 [2, 3072], P(None, 'tensor'), may hold values from -3 to 3
- shrink_matrices: bfloat16 [2, 3072, 768], P(None, 'tensor'), may hold values from -0.109375 to 0.109375
- shrink_offsets: bfloat16 [2, 768], replicated, may hold values from -3 to 3
- standardize_factors: bfloat16 [4, 768], replicated, may hold values from 0.5 to 1.5
- standardize_shifts: bfloat16 [4, 768], replicated, may hold values from -2 to 2
- matching_projectors: bfloat16 [2, 768, 256], replicated, may hold values from -0.21875 to 0.21875
- matching_offsets: bfloat16 [2, 256], replicated, may hold values from -2 to 2
- softness_factor: float32 [1], replicated, may hold values from 0.03 to 0.1
- result_cotangent: bfloat16 [64, 64, 768], P('dp'), may hold values from -6 to 6
Outputs:
- layer_output: bfloat16 [64, 64, 768], P('dp')
- hidden_grad: bfloat16 [64, 64, 768], P('dp')
- loss_value: float32 [1], replicated
- self_weights_grad: float32 [768, 3, 768], P('dp', None, 'tensor')
- self_biases_grad: float32 [2, 768], P(None, 'tensor')
- self_output_grad: float32 [768, 768], P('tensor', 'dp')
- self_shift_grad: float32 [768], replicated
- cross_query_grad: float32 [768, 768], P('dp', 'tensor')
- cross_image_grad: float32 [1408, 2, 768], P('dp', None, 'tensor')
- cross_biases_grad: float32 [2, 768], P(None, 'tensor')
- cross_output_grad: float32 [768, 768], P('tensor', 'dp')
- cross_shift_grad: float32 [768], replicated
- expand_weights_grad: float32 [2, 768, 3072], P(None, 'dp', 'tensor')
- expand_biases_grad: float32 [2, 3072], P(None, 'tensor')
- reduce_weights_grad: float32 [2, 3072, 768], P(None, 'tensor', 'dp')
- reduce_biases_grad: float32 [2, 768], replicated
- norm_gains_grad: float32 [4, 768], replicated
- norm_shifts_grad: float32 [4, 768], replicated
- contrast_weights_grad: float32 [2, 768, 256], P(None, 'dp')
- contrast_biases_grad: float32 [2, 256], replicated
- softness_sensitivity: float32 [1], replicated
The draws below stay inside these ranges and needn't reach their ends.
Inputs may be any that keep to these rules, and one draw needn't show every extreme that they name: `caption_sizes`: each caption has 5 to 32 tokens; the first item's caption has 32 and the second's 5.
All inputs are finite; a program needn't handle non-finite values.
Results may differ from the reference program's by a relative error of at most 0.028.
Values may be sent and summed in bfloat16 or wider, within the bound.
No kernel may reach another device: no remote copies, remote signals or barrier semaphores. Data moves between devices by JAX's collectives and lax.ppermute only.
A program may use at most 128 MiB of HBM per device.

```python
import math
import jax
import jax.numpy as jnp
from jax import lax

D = 768
HEADS = 12
HD = 64
FF = 3072
VD = 1408
NV = 257
LEARNED_ROWS = 32
NT = 32
MIN_LEN = 5
EMBED_WIDTH = 256
SAMPLE_TOTAL = 64


def draw_caption_sizes(key, part):
    drawn_lengths = jax.random.randint(key, (SAMPLE_TOTAL,), MIN_LEN, NT + 1, dtype=jnp.int32)
    return drawn_lengths.at[0].set(NT).at[1].set(MIN_LEN)


def level_of(key, extent, shards, smallest, largest):
    level, own = 1.0, jax.random.fold_in(key, 6)
    for axis_at, shards_of in shards:
        steps = jnp.exp(jax.random.uniform(jax.random.fold_in(own, axis_at), (shards_of,), jnp.float32, smallest / len(shards), largest / len(shards)))
        level = level * jnp.repeat(steps, extent[axis_at] // shards_of).reshape([-1 if axis == axis_at else 1 for axis in range(len(extent))])
    return level


def bell_draw(key, extent, scale, bound, pieces=(), held_as=jnp.bfloat16):
    drawn = scale * jax.random.normal(key, extent, jnp.float32)
    if pieces:
        drawn = drawn * level_of(key, extent, pieces, -0.22, 0.18)
    return jnp.clip(drawn, -bound, bound).astype(held_as)


def setup_inputs(seed: int = 0) -> dict:
    key_of = jax.random.split(jax.random.key(seed), 23)
    layer_entry_rows = bell_draw(key_of[0], (SAMPLE_TOTAL, LEARNED_ROWS + NT, D), 1.0, 6.0, ((0, 8),))
    frozen_picture_features = bell_draw(key_of[1], (SAMPLE_TOTAL, NV, VD), 1.0, 6.0, ((0, 8),))
    caption_sizes = draw_caption_sizes(jax.random.fold_in(key_of[22], 71), 0)
    inner_attend_projectors = bell_draw(key_of[3], (D, 3, D), D ** -0.5, 0.21875, ((2, 4),))
    inner_attend_offsets = bell_draw(key_of[4], (2, D), 0.5, 3.0, ((1, 4),))
    inner_attend_exit_matrix = bell_draw(key_of[5], (D, D), (D // 16) ** -0.5, 0.875, ((0, 4),))
    inner_attend_exit_offset = bell_draw(key_of[6], (D,), 0.5, 3.0)
    mutual_attend_probe_matrix = bell_draw(key_of[7], (D, D), D ** -0.5, 0.21875, ((1, 4),))
    picture_keyvalue_matrix = bell_draw(key_of[8], (VD, 2, D), VD ** -0.5, 0.15625, ((2, 4),))
    mutual_attend_offsets = bell_draw(key_of[9], (2, D), 0.5, 3.0, ((1, 4),))
    mutual_attend_exit_matrix = bell_draw(key_of[10], (D, D), (D // 64) ** -0.5, 1.75, ((0, 4),))
    mutual_attend_exit_offset = bell_draw(key_of[11], (D,), 0.5, 3.0)
    expansion_matrices = bell_draw(key_of[12], (2, D, FF), D ** -0.5, 0.21875, ((2, 4),))
    expansion_offsets = bell_draw(key_of[13], (2, FF), 0.5, 3.0, ((1, 4),))
    shrink_matrices = bell_draw(key_of[14], (2, FF, D), FF ** -0.5, 0.109375, ((1, 4),))
    shrink_offsets = bell_draw(key_of[15], (2, D), 0.5, 3.0)
    standardize_factors = jnp.clip(1.0 + 0.1 * jax.random.normal(key_of[16], (4, D), jnp.float32), 0.5, 1.5).astype(jnp.bfloat16)
    standardize_shifts = bell_draw(key_of[17], (4, D), 0.3, 2.0)
    matching_projectors = bell_draw(key_of[18], (2, D, EMBED_WIDTH), D ** -0.5, 0.21875)
    matching_offsets = bell_draw(key_of[19], (2, EMBED_WIDTH), 0.3, 2.0)
    softness_factor = jnp.clip(jnp.exp(jax.random.uniform(key_of[20], (1,), jnp.float32, math.log(0.03), math.log(0.1))), 0.03, 0.1)
    result_cotangent = bell_draw(key_of[21], (SAMPLE_TOTAL, LEARNED_ROWS + NT, D), 1.0, 6.0, ((0, 8),))
    return dict(layer_entry_rows=layer_entry_rows, frozen_picture_features=frozen_picture_features, caption_sizes=caption_sizes, inner_attend_projectors=inner_attend_projectors, inner_attend_offsets=inner_attend_offsets, inner_attend_exit_matrix=inner_attend_exit_matrix, inner_attend_exit_offset=inner_attend_exit_offset, mutual_attend_probe_matrix=mutual_attend_probe_matrix, picture_keyvalue_matrix=picture_keyvalue_matrix, mutual_attend_offsets=mutual_attend_offsets, mutual_attend_exit_matrix=mutual_attend_exit_matrix, mutual_attend_exit_offset=mutual_attend_exit_offset, expansion_matrices=expansion_matrices, expansion_offsets=expansion_offsets, shrink_matrices=shrink_matrices, shrink_offsets=shrink_offsets, standardize_factors=standardize_factors, standardize_shifts=standardize_shifts, matching_projectors=matching_projectors, matching_offsets=matching_offsets, softness_factor=softness_factor, result_cotangent=result_cotangent)


@jax.custom_vjp
def low(v):
    return lax.optimization_barrier(v.astype(jnp.bfloat16)).astype(jnp.float32)

@jax.custom_vjp
def low_back(v):
    return v

def low_keep(v):
    return (low(v), None)

def low_pass(kept, grad):
    return (grad,)

def back_keep(v):
    return (v, None)

def back_low(kept, grad):
    return (low(grad),)
low.defvjp(low_keep, low_pass)
low_back.defvjp(back_keep, back_low)
peak_value = lax.Precision.HIGHEST
masked_score = -1000000000.0

def both_ways(v):
    return low_back(low(v))

def matmul(a, b):
    return jnp.dot(a, b, precision=peak_value, preferred_element_type=jnp.float32)

def layer_norm(v, g, b):
    average = lax.optimization_barrier(jnp.mean(v, axis=-1, keepdims=True))
    centered = v - average
    spread = lax.optimization_barrier(jnp.mean(centered * centered, axis=-1, keepdims=True))
    return centered * lax.rsqrt(spread + 1e-06) * g + b

def unit_rows(z):
    return z * lax.rsqrt(lax.optimization_barrier(jnp.sum(z * z, axis=-1, keepdims=True)) + 1e-06)

def gelu_exact(u):
    return jax.nn.gelu(u, approximate=False)

def self_mask(caption_sizes, row_width):
    positions = jnp.arange(row_width, dtype=jnp.int32)
    is_query = positions < LEARNED_ROWS
    text_valid = positions[None, :] - LEARNED_ROWS < caption_sizes[:, None]
    key_valid = is_query[None, :] | text_valid
    same_side = is_query[:, None] == is_query[None, :]
    return same_side[None, None] & key_valid[:, None, None, :]

def split_heads(t, count, length):
    return t.reshape(count, length, HEADS, HD)

def attend(q, k, v, allowed):
    scores = low_back(jnp.einsum('gihd,gjhd->ghij', q, k, precision=peak_value) * HD ** (-0.5))
    if allowed is not None:
        scores = jnp.where(allowed, scores, masked_score)
    row_peak = lax.optimization_barrier(jnp.max(scores, axis=-1, keepdims=True))
    exp_terms = jnp.exp(scores - row_peak)
    attn_probs = exp_terms / lax.optimization_barrier(jnp.sum(exp_terms, axis=-1, keepdims=True))
    return both_ways(jnp.einsum('ghij,gjhd->gihd', low(attn_probs), v, precision=peak_value))

def feed_forward(learnables, inputs, which):
    expansion_matrices, expansion_offsets, shrink_matrices, shrink_offsets, standardize_factors, standardize_shifts = learnables[9:15]
    pre_act = low_back(matmul(low(inputs), expansion_matrices[which]) + expansion_offsets[which])
    activation = low(gelu_exact(pre_act))
    result = low_back(matmul(activation, shrink_matrices[which]) + shrink_offsets[which])
    return layer_norm(inputs + result, standardize_factors[2 + which], standardize_shifts[2 + which])

def layer_items(learnables, rows, pics, lens):
    inner_attend_projectors, inner_attend_offsets, inner_attend_exit_matrix, inner_attend_exit_offset, mutual_attend_probe_matrix, picture_keyvalue_matrix, mutual_attend_offsets, mutual_attend_exit_matrix, mutual_attend_exit_offset = learnables[:9]
    standardize_factors = learnables[13]
    standardize_shifts = learnables[14]
    matching_projectors = learnables[15]
    matching_offsets = learnables[16]
    sample_tally = rows.shape[0]
    row_width = LEARNED_ROWS + NT
    flat_rows = rows.reshape(sample_tally * row_width, D)
    projected = jnp.einsum('rd,dtk->rtk', flat_rows, inner_attend_projectors, precision=peak_value)
    queries = both_ways(projected[:, 0] + inner_attend_offsets[0])
    keys_self = both_ways(projected[:, 1])
    values_self = both_ways(projected[:, 2] + inner_attend_offsets[1])
    mixed_self = attend(split_heads(queries, sample_tally, row_width), split_heads(keys_self, sample_tally, row_width), split_heads(values_self, sample_tally, row_width), self_mask(lens, row_width))
    attn_out = low_back(matmul(mixed_self.reshape(sample_tally * row_width, D), inner_attend_exit_matrix) + inner_attend_exit_offset)
    first_norm = layer_norm(flat_rows + attn_out, standardize_factors[0], standardize_shifts[0]).reshape(sample_tally, row_width, D)
    query_rows = first_norm[:, :LEARNED_ROWS].reshape(sample_tally * LEARNED_ROWS, D)
    text_rows = first_norm[:, LEARNED_ROWS:].reshape(sample_tally * NT, D)
    cross_q = both_ways(matmul(low(query_rows), mutual_attend_probe_matrix) + mutual_attend_offsets[0])
    image_rows = pics.astype(jnp.float32).reshape(sample_tally * NV, VD)
    cross_kv = jnp.einsum('rv,vtk->rtk', image_rows, picture_keyvalue_matrix, precision=peak_value)
    cross_k = both_ways(cross_kv[:, 0])
    cross_v = both_ways(cross_kv[:, 1] + mutual_attend_offsets[1])
    mixed_cross = attend(split_heads(cross_q, sample_tally, LEARNED_ROWS), split_heads(cross_k, sample_tally, NV), split_heads(cross_v, sample_tally, NV), None)
    cross_out = low_back(matmul(mixed_cross.reshape(sample_tally * LEARNED_ROWS, D), mutual_attend_exit_matrix) + mutual_attend_exit_offset)
    second = layer_norm(query_rows + cross_out, standardize_factors[1], standardize_shifts[1])
    query_final = feed_forward(learnables, second, 0)
    text_final = feed_forward(learnables, text_rows, 1)
    finals = jnp.concatenate([query_final.reshape(sample_tally, LEARNED_ROWS, D), text_final.reshape(sample_tally, NT, D)], axis=1)
    image_pre = low_back(matmul(low(query_final), matching_projectors[0]) + matching_offsets[0])
    picture_vector = low(unit_rows(image_pre)).reshape(sample_tally, LEARNED_ROWS, EMBED_WIDTH)
    caption_rows = text_final.reshape(sample_tally, NT, D)[:, 0]
    caption_pre = low_back(matmul(low(caption_rows), matching_projectors[1]) + matching_offsets[1])
    sentence_vector = low(unit_rows(caption_pre))
    return (finals, picture_vector, sentence_vector)

def pairing_match(picture_vector, sentence_vector, log_softness):
    multiplied_values = low_back(jnp.einsum('yvg,dg->yvd', picture_vector, sentence_vector, precision=peak_value)) / log_softness[0]
    query_peak = lax.optimization_barrier(jnp.max(multiplied_values, axis=1, keepdims=True))
    logits = query_peak[:, 0] + jnp.log(lax.optimization_barrier(jnp.sum(jnp.exp(multiplied_values - query_peak), axis=1)))
    row_peak = lax.optimization_barrier(jnp.max(logits, axis=1, keepdims=True))
    row_lse = row_peak[:, 0] + jnp.log(lax.optimization_barrier(jnp.sum(jnp.exp(logits - row_peak), axis=1)))
    col_peak = lax.optimization_barrier(jnp.max(logits, axis=0, keepdims=True))
    col_lse = col_peak[0] + jnp.log(lax.optimization_barrier(jnp.sum(jnp.exp(logits - col_peak), axis=0)))
    diagonal_logits = jnp.diagonal(logits)
    return (jnp.sum(row_lse - diagonal_logits) + jnp.sum(col_lse - diagonal_logits)) / (2.0 * SAMPLE_TOTAL)

def reference(layer_entry_rows, frozen_picture_features, caption_sizes, inner_attend_projectors, inner_attend_offsets, inner_attend_exit_matrix, inner_attend_exit_offset, mutual_attend_probe_matrix, picture_keyvalue_matrix, mutual_attend_offsets, mutual_attend_exit_matrix, mutual_attend_exit_offset, expansion_matrices, expansion_offsets, shrink_matrices, shrink_offsets, standardize_factors, standardize_shifts, matching_projectors, matching_offsets, softness_factor, result_cotangent):
    learnable_collection = tuple((w.astype(jnp.float32) for w in (inner_attend_projectors, inner_attend_offsets, inner_attend_exit_matrix, inner_attend_exit_offset, mutual_attend_probe_matrix, picture_keyvalue_matrix, mutual_attend_offsets, mutual_attend_exit_matrix, mutual_attend_exit_offset, expansion_matrices, expansion_offsets, shrink_matrices, shrink_offsets, standardize_factors, standardize_shifts, matching_projectors, matching_offsets)))
    group_size = math.gcd(SAMPLE_TOTAL, 64)
    groups = SAMPLE_TOTAL // group_size
    pics = frozen_picture_features.reshape(groups, group_size, NV, VD)
    lens = caption_sizes.reshape(groups, group_size)
    cotangent = result_cotangent.astype(jnp.float32)

    def fitting_criterion(learnables, incoming_lines, log_softness):

        def one_group(block):
            return layer_items(learnables, block[0], block[1], block[2])
        finals, picture_vector, sentence_vector = lax.map(jax.checkpoint(one_group), (incoming_lines.reshape(groups, group_size, LEARNED_ROWS + NT, D), pics, lens))
        outputs = finals.reshape(SAMPLE_TOTAL, LEARNED_ROWS + NT, D)
        penalty_value = pairing_match(picture_vector.reshape(SAMPLE_TOTAL, LEARNED_ROWS, EMBED_WIDTH), sentence_vector.reshape(SAMPLE_TOTAL, EMBED_WIDTH), log_softness)
        return (jnp.sum(outputs * cotangent) + penalty_value, (outputs, penalty_value))
    penalty_number, reverse_mode_rule, side_returns = jax.vjp(fitting_criterion, learnable_collection, layer_entry_rows.astype(jnp.float32), softness_factor, has_aux=True)
    weight_grads, input_grad, temper_grad = reverse_mode_rule(jnp.ones((), jnp.float32))
    g_sw, g_sb, g_so, g_ss, g_cq, g_ci, g_cb, g_co, g_cs, g_ew, g_eb, g_rw, g_rb, g_ng, g_ns, g_pw, g_pb = weight_grads
    return (side_returns[0].astype(jnp.bfloat16), input_grad.astype(jnp.bfloat16), side_returns[1].reshape(1), g_sw, g_sb, g_so, g_ss, g_cq, g_ci, g_cb, g_co, g_cs, g_ew, g_eb, g_rw, g_rb, g_ng, g_ns, g_pw, g_pb, temper_grad)
```

```python
import jax
import jax.numpy as jnp
from jax import lax
from jax.sharding import PartitionSpec as P

D = 768
HD = 64
VD = 1408
NV = 257
LEARNED_ROWS = 32
NT = 32


masked_score = -1000000000.0
low_type = jnp.bfloat16
wide_type = jnp.float32


def swap(part, axis, bit):
    size = lax.axis_size(axis)
    return lax.ppermute(part, axis, [(i, i ^ bit) for i in range(size)])


def axis_bits(axis):
    size = lax.axis_size(axis)
    assert size & (size - 1) == 0
    return [1 << k for k in range(size.bit_length() - 1)]


def own_bit(axis, bit):
    return (lax.axis_index(axis) // bit) % 2


def tensor_total(part):
    bits = axis_bits("tensor")
    if not bits:
        return part
    half = part.shape[0] // 2
    mine = own_bit("tensor", 1)
    keep = lax.dynamic_slice_in_dim(part, mine * half, half)
    away = lax.dynamic_slice_in_dim(part, (1 - mine) * half, half).astype(low_type)
    total = keep + swap(away, "tensor", 1).astype(wide_type)
    low = total.astype(low_type)
    for bit in bits[1:]:
        low = (low.astype(wide_type) + swap(low, "tensor", bit).astype(wide_type)).astype(low_type)
    other = swap(low, "tensor", 1)
    first = jnp.where(mine == 0, low, other)
    second = jnp.where(mine == 0, other, low)
    return jnp.concatenate([first, second], axis=0).astype(wide_type)


def dp_scatter(part, send_type=low_type):
    count = lax.axis_size("dp")
    total = part.reshape((count, part.shape[0] // count) + part.shape[1:])
    for bit in axis_bits("dp"):
        paired = total.reshape((total.shape[0] // 2, 2) + total.shape[1:])
        mine = own_bit("dp", bit)
        keep = lax.dynamic_index_in_dim(paired, mine, 1, keepdims=False)
        away = lax.dynamic_index_in_dim(paired, 1 - mine, 1, keepdims=False).astype(send_type)
        total = keep + swap(away, "dp", bit).astype(wide_type)
    return total[0]


def dp_total(part):
    for bit in axis_bits("dp"):
        part = part + swap(part, "dp", bit)
    return part


def dp_gather(part):
    whole = part[None]
    for bit in axis_bits("dp"):
        other = swap(whole, "dp", bit)
        mine = own_bit("dp", bit)
        first = jnp.where(mine == 0, whole, other)
        second = jnp.where(mine == 0, other, whole)
        whole = jnp.concatenate([first, second], axis=0)
    return whole.reshape((-1,) + part.shape[1:])


def layer_norm_parts(v):
    centered = v - jnp.mean(v, axis=-1, keepdims=True)
    scale = lax.rsqrt(jnp.mean(centered * centered, axis=-1, keepdims=True) + 1e-06)
    return centered * scale, scale


def norm_back(unit, scale, g, grad_out):
    h = grad_out * g
    grad_in = scale * (
        h - jnp.mean(h, axis=-1, keepdims=True) - unit * jnp.mean(h * unit, axis=-1, keepdims=True)
    )
    return grad_in, jnp.sum(grad_out * unit, axis=0), jnp.sum(grad_out, axis=0)


def unit_scale(z):
    return lax.rsqrt(jnp.sum(z * z, axis=-1, keepdims=True) + 1e-06)


def gelu_pair(u):
    phi = 0.5 * (1.0 + lax.erf(u * 0.7071067811865476))
    slope = phi + u * jnp.exp(-0.5 * u * u) * 0.3989422804014327
    return u * phi, slope


def score_block(q, k, allowed):
    scores = jnp.einsum("gihd,gjhd->ghij", q, k, preferred_element_type=wide_type) * HD ** (-0.5)
    if allowed is not None:
        scores = jnp.where(allowed, scores, masked_score)
    return scores


def attend_forward(q, k, v, allowed):
    scores = score_block(q, k, allowed)
    exp_terms = jnp.exp(scores - jnp.max(scores, axis=-1, keepdims=True))
    probs = exp_terms / jnp.sum(exp_terms, axis=-1, keepdims=True)
    mixed = jnp.einsum("ghij,gjhd->gihd", probs.astype(low_type), v, preferred_element_type=wide_type)
    return mixed.astype(low_type), probs


def attend_backward(q, k, v, probs, grad_mixed):
    grad_probs = jnp.einsum("gihd,gjhd->ghij", grad_mixed, v, preferred_element_type=wide_type)
    grad_v = jnp.einsum(
        "ghij,gihd->gjhd", probs.astype(low_type), grad_mixed, preferred_element_type=wide_type
    )
    inner_sum = jnp.sum(probs * grad_probs, axis=-1, keepdims=True)
    grad_scores = (probs * (grad_probs - inner_sum)).astype(low_type)
    grad_q = jnp.einsum("ghij,gjhd->gihd", grad_scores, k, preferred_element_type=wide_type) * HD ** (-0.5)
    grad_k = jnp.einsum("ghij,gihd->gjhd", grad_scores, q, preferred_element_type=wide_type) * HD ** (-0.5)
    return grad_q.astype(low_type), grad_k.astype(low_type), grad_v.astype(low_type)


def mm(a, b):
    return jnp.dot(a, b, preferred_element_type=wide_type)


def mm_nt(a, b):
    return jnp.einsum("ik,jk->ij", a, b, preferred_element_type=wide_type)


def mm_tn(a, b):
    return jnp.einsum("ki,kj->ij", a, b, preferred_element_type=wide_type)


def local(
    layer_entry_rows,
    frozen_picture_features,
    caption_sizes,
    inner_attend_projectors,
    inner_attend_offsets,
    inner_attend_exit_matrix,
    inner_attend_exit_offset,
    mutual_attend_probe_matrix,
    picture_keyvalue_matrix,
    mutual_attend_offsets,
    mutual_attend_exit_matrix,
    mutual_attend_exit_offset,
    expansion_matrices,
    expansion_offsets,
    shrink_matrices,
    shrink_offsets,
    standardize_factors,
    standardize_shifts,
    matching_projectors,
    matching_offsets,
    softness_factor,
    result_cotangent,
):
    items = layer_entry_rows.shape[0]
    width = inner_attend_projectors.shape[2]
    heads = width // HD
    count = items * LEARNED_ROWS
    gains = standardize_factors.astype(wide_type)
    shifts = standardize_shifts.astype(wide_type)

    def grouped(t):
        return jnp.concatenate(
            [t[:, :LEARNED_ROWS].reshape(count, D), t[:, LEARNED_ROWS:].reshape(count, D)], axis=0
        )

    def ungrouped(t):
        return jnp.concatenate(
            [t[:count].reshape(items, LEARNED_ROWS, D), t[count:].reshape(items, NT, D)], axis=1
        )

    rows = grouped(layer_entry_rows)
    w_qkv = inner_attend_projectors.reshape(D, 3 * width)
    projected = mm(rows, w_qkv)
    blocks = 2 * items

    def split(t, length):
        return t.reshape(-1, length, heads, HD)

    sq = split((projected[:, :width] + inner_attend_offsets[0]).astype(low_type), NT)
    sk = split(projected[:, width : 2 * width].astype(low_type), NT)
    sv = split((projected[:, 2 * width :] + inner_attend_offsets[1]).astype(low_type), NT)
    valid = jnp.concatenate([jnp.full((items,), NT, jnp.int32), caption_sizes])
    allowed = jnp.arange(NT, dtype=jnp.int32)[None, None, None, :] < valid[:, None, None, None]
    mixed, probs = attend_forward(sq, sk, sv, allowed)
    mixed = mixed.reshape(2 * count, width)
    attn_out = tensor_total(mm(mixed, inner_attend_exit_matrix)) + inner_attend_exit_offset
    unit0, scale0 = layer_norm_parts(rows.astype(wide_type) + attn_out)
    first = unit0 * gains[0] + shifts[0]
    query_rows = first[:count]
    text_rows = first[count:]
    query_low = query_rows.astype(low_type)
    text_low = text_rows.astype(low_type)

    w_kv = picture_keyvalue_matrix.reshape(VD, 2 * width)
    cross_kv = jnp.einsum("gnv,vk->gnk", frozen_picture_features, w_kv, preferred_element_type=wide_type)
    ck = cross_kv[..., :width].astype(low_type).reshape(items, NV, heads, HD)
    cv = (cross_kv[..., width:] + mutual_attend_offsets[1]).astype(low_type).reshape(items, NV, heads, HD)
    cq = split((mm(query_low, mutual_attend_probe_matrix) + mutual_attend_offsets[0]).astype(low_type), LEARNED_ROWS)
    cross_mixed, cross_probs = attend_forward(cq, ck, cv, None)
    cross_flat = cross_mixed.reshape(count, width)
    cross_out = tensor_total(mm(cross_flat, mutual_attend_exit_matrix)) + mutual_attend_exit_offset
    unit1, scale1 = layer_norm_parts(query_rows + cross_out)
    second = unit1 * gains[1] + shifts[1]
    second_low = second.astype(low_type)

    def feed(which, values, values_low):
        pre = mm(values_low, expansion_matrices[which]) + expansion_offsets[which]
        act, slope = gelu_pair(pre)
        act = act.astype(low_type)
        total = tensor_total(mm(act, shrink_matrices[which]))
        unit, scale = layer_norm_parts(values + (total + shrink_offsets[which]))
        return act, slope, unit, scale, unit * gains[2 + which] + shifts[2 + which]

    act_t, slope_t, unit3, scale3, text_final = feed(1, text_rows, text_low)
    act_q, slope_q, unit2, scale2, query_final = feed(0, second, second_low)
    final_low = query_final.astype(low_type)
    text_final_low = text_final.astype(low_type)
    layer_output = ungrouped(jnp.concatenate([final_low, text_final_low], axis=0))

    caption_low = text_final_low.reshape(items, NT, D)[:, 0]
    caption_pre = mm(caption_low, matching_projectors[1]) + matching_offsets[1]
    caption_scale = unit_scale(caption_pre)
    sentence_unit = caption_pre * caption_scale
    all_captions = dp_gather(sentence_unit.astype(low_type))
    tally = all_captions.shape[0]
    image_pre = mm(final_low, matching_projectors[0]) + matching_offsets[0]
    image_scale = unit_scale(image_pre)
    picture_unit = image_pre * image_scale
    picture_low = picture_unit.astype(low_type)
    softness = softness_factor[0]
    scaled = (mm_nt(picture_low, all_captions) / softness).reshape(items, LEARNED_ROWS, tally)
    query_peak = jnp.max(scaled, axis=1, keepdims=True)
    query_exp = jnp.exp(scaled - query_peak)
    query_total = jnp.sum(query_exp, axis=1, keepdims=True)
    logits = query_peak[:, 0] + jnp.log(query_total[:, 0])
    share = query_exp / query_total
    exp_logits = jnp.exp(logits)
    row_total = jnp.sum(exp_logits, axis=1, keepdims=True)
    col_total = dp_total(jnp.sum(exp_logits, axis=0))
    offset = lax.axis_index("dp") * items
    own_pair = (
        jnp.arange(tally, dtype=jnp.int32)[None, :]
        == (offset + jnp.arange(items, dtype=jnp.int32))[:, None]
    )
    inverse = 1.0 / (2.0 * tally)
    own_terms = jnp.where(own_pair, jnp.log(col_total)[None, :] - 2.0 * logits, 0.0)
    loss_local = (jnp.sum(jnp.log(row_total)) + jnp.sum(own_terms)) * inverse
    grad_logits = (
        exp_logits / row_total + exp_logits / col_total[None, :] - jnp.where(own_pair, 2.0, 0.0)
    ) * inverse
    grad_scaled = grad_logits[:, None, :] * share
    softness_here = -jnp.sum(grad_scaled * scaled) / softness
    grad_dots = (grad_scaled / softness).astype(low_type).reshape(count, tally)
    grad_image_feat = mm(grad_dots, all_captions)
    caption_part = mm_tn(grad_dots, picture_low)
    grad_caption_feat = dp_scatter(caption_part, wide_type)

    def unit_back(unit, scale, grad):
        return ((grad - unit * jnp.sum(unit * grad, axis=-1, keepdims=True)) * scale).astype(low_type)

    grad_image_pre = unit_back(picture_unit, image_scale, grad_image_feat)
    grad_caption_pre = unit_back(sentence_unit, caption_scale, grad_caption_feat)
    match_grad = jnp.concatenate(
        [mm_tn(final_low, grad_image_pre), mm_tn(caption_low, grad_caption_pre)], axis=1
    )
    match_bias = [
        jnp.sum(grad_image_pre, axis=0, dtype=wide_type),
        jnp.sum(grad_caption_pre, axis=0, dtype=wide_type),
    ]
    grad_query_final = result_cotangent[:, :LEARNED_ROWS].reshape(count, D).astype(wide_type) + mm_nt(
        grad_image_pre, matching_projectors[0]
    )
    grad_first_token = mm_nt(grad_caption_pre, matching_projectors[1])
    grad_text_final = (
        result_cotangent[:, LEARNED_ROWS:].astype(wide_type)
        + jnp.where(jnp.arange(NT)[None, :, None] == 0, grad_first_token[:, None, :], 0.0)
    ).reshape(count, D)

    def feed_back(which, grad_out, unit, scale, values_low, act, slope):
        grad_in, gain, shift = norm_back(unit, scale, gains[2 + which], grad_out)
        grad_low = grad_in.astype(low_type)
        grad_pre = (mm_nt(grad_low, shrink_matrices[which]) * slope).astype(low_type)
        back = grad_in + tensor_total(mm_nt(grad_pre, expansion_matrices[which]))
        reduce_grad = mm_tn(grad_low, act)
        expand_grad = mm_tn(values_low, grad_pre)
        return (
            back,
            gain,
            shift,
            reduce_grad,
            jnp.sum(grad_low, axis=0, dtype=wide_type),
            expand_grad,
            jnp.sum(grad_pre, axis=0, dtype=wide_type),
        )

    grad_second, gain2, shift2, rw_q, rb_q, ew_q, eb_q = feed_back(
        0, grad_query_final, unit2, scale2, second_low, act_q, slope_q
    )
    grad_text_rows, gain3, shift3, rw_t, rb_t, ew_t, eb_t = feed_back(
        1, grad_text_final, unit3, scale3, text_low, act_t, slope_t
    )

    grad_second_in, gain1, shift1 = norm_back(unit1, scale1, gains[1], grad_second)
    grad_cross_out = grad_second_in.astype(low_type)
    cross_output = mm_tn(grad_cross_out, cross_flat)
    cross_shift = jnp.sum(grad_cross_out, axis=0, dtype=wide_type)
    grad_cross_mixed = split(mm_nt(grad_cross_out, mutual_attend_exit_matrix).astype(low_type), LEARNED_ROWS)
    grad_cq, grad_ck, grad_cv = attend_backward(cq, ck, cv, cross_probs, grad_cross_mixed)
    grad_cq = grad_cq.reshape(count, width)
    grad_ckv = jnp.concatenate(
        [grad_ck.reshape(items, NV, width), grad_cv.reshape(items, NV, width)], axis=2
    )
    cross_query = mm_tn(query_low, grad_cq)
    cross_image = jnp.einsum("gnv,gnk->vk", frozen_picture_features, grad_ckv, preferred_element_type=wide_type)
    cross_bias = [
        jnp.sum(grad_cq, axis=0, dtype=wide_type),
        jnp.sum(grad_ckv[..., width:], axis=(0, 1), dtype=wide_type),
    ]
    grad_query_rows = grad_second_in + tensor_total(mm_nt(grad_cq, mutual_attend_probe_matrix))

    grad_first = jnp.concatenate([grad_query_rows, grad_text_rows], axis=0)
    grad_first_in, gain0, shift0 = norm_back(unit0, scale0, gains[0], grad_first)
    grad_attn_out = grad_first_in.astype(low_type)
    self_output = mm_tn(grad_attn_out, mixed)
    self_shift = jnp.sum(grad_attn_out, axis=0, dtype=wide_type)
    grad_mixed = split(mm_nt(grad_attn_out, inner_attend_exit_matrix).astype(low_type), NT)
    grad_sq, grad_sk, grad_sv = attend_backward(sq, sk, sv, probs, grad_mixed)
    grad_qkv = jnp.concatenate([t.reshape(2 * count, width) for t in (grad_sq, grad_sk, grad_sv)], axis=1)
    self_weights = mm_tn(rows, grad_qkv)
    self_bias = [
        jnp.sum(grad_qkv[:, :width], axis=0, dtype=wide_type),
        jnp.sum(grad_qkv[:, 2 * width :], axis=0, dtype=wide_type),
    ]
    input_back = tensor_total(mm_nt(grad_qkv, w_qkv))
    hidden_grad = ungrouped((grad_first_in + input_back).astype(low_type))

    wide = expansion_matrices.shape[2]
    feed_grads = dp_scatter(jnp.concatenate([rw_q, rw_t, ew_q, ew_t, match_grad], axis=1))
    cross_grads = dp_scatter(jnp.concatenate([cross_output, cross_query], axis=1))
    image_grads = dp_scatter(cross_image)
    self_grads = dp_scatter(jnp.concatenate([self_output, self_weights], axis=1))
    g_rw = jnp.stack([feed_grads[:, :wide].T, feed_grads[:, wide : 2 * wide].T])
    g_ew = jnp.stack([feed_grads[:, 2 * wide : 3 * wide], feed_grads[:, 3 * wide : 4 * wide]])
    embed = matching_projectors.shape[2]
    g_pw = jnp.stack([feed_grads[:, 4 * wide : 4 * wide + embed], feed_grads[:, 4 * wide + embed :]])
    g_co = cross_grads[:, :width].T
    g_cq = cross_grads[:, width:]
    g_ci = image_grads.reshape(-1, 2, width)
    g_so = self_grads[:, :width].T
    g_sw = self_grads[:, width:].reshape(-1, 3, width)

    small = [
        jnp.concatenate(self_bias),
        self_shift,
        jnp.concatenate(cross_bias),
        cross_shift,
        jnp.concatenate([eb_q, eb_t]),
        jnp.concatenate([rb_q, rb_t]),
        jnp.concatenate([gain0, gain1, gain2, gain3]),
        jnp.concatenate([shift0, shift1, shift2, shift3]),
        jnp.concatenate(match_bias),
        jnp.reshape(loss_local, (1,)),
        jnp.reshape(softness_here, (1,)),
    ]
    sizes = [t.shape[0] for t in small]
    packed = jnp.concatenate(small)
    pad = -packed.shape[0] % 1024
    packed = dp_total(jnp.pad(packed, (0, pad)).reshape(-1, 128)).reshape(-1)
    parts, at = [], 0
    for size in sizes:
        parts.append(packed[at : at + size])
        at += size
    g_sb, g_ss, g_cb, g_cs, g_eb, g_rb, g_ng, g_ns, g_pb, loss_value, softness_sensitivity = parts
    return (
        layer_output,
        hidden_grad,
        loss_value,
        g_sw,
        g_sb.reshape(2, -1),
        g_so,
        g_ss,
        g_cq,
        g_ci,
        g_cb.reshape(2, -1),
        g_co,
        g_cs,
        g_ew,
        g_eb.reshape(2, -1),
        g_rw,
        g_rb.reshape(2, -1),
        g_ng.reshape(4, -1),
        g_ns.reshape(4, -1),
        g_pw,
        g_pb.reshape(2, -1),
        softness_sensitivity,
    )


def solution(mesh):
    return jax.shard_map(
        local,
        mesh=mesh,
        in_specs=(
            P("dp", None, None),
            P("dp", None, None),
            P("dp"),
            P(None, None, "tensor"),
            P(None, "tensor"),
            P("tensor", None),
            P(),
            P(None, "tensor"),
            P(None, None, "tensor"),
            P(None, "tensor"),
            P("tensor", None),
            P(),
            P(None, None, "tensor"),
            P(None, "tensor"),
            P(None, "tensor", None),
            P(),
            P(),
            P(),
            P(),
            P(),
            P(),
            P("dp", None, None),
        ),
        out_specs=(
            P("dp", None, None),
            P("dp", None, None),
            P(),
            P("dp", None, "tensor"),
            P(None, "tensor"),
            P("tensor", "dp"),
            P(),
            P("dp", "tensor"),
            P("dp", None, "tensor"),
            P(None, "tensor"),
            P("tensor", "dp"),
            P(),
            P(None, "dp", "tensor"),
            P(None, "tensor"),
            P(None, "tensor", "dp"),
            P(),
            P(),
            P(),
            P(None, "dp", None),
            P(),
            P(),
        ),
        check_vma=False,
    )
```
